32 devices in a mesh: parts: 2 (over x), tok: 16 (over z, y, core).
Axes of the slice: x: 2, y: 2, z: 4, core: 2. Of those that a mesh axis runs over, the one named last changes fastest.
Arguments:
- queries: bfloat16 [4096, 4096], P(('parts', 'tok')), parts along dimension 0, may hold values from -30 to 30
- keys: bfloat16 [4096, 512], P(('parts', 'tok')), parts along dimension 0, may hold values from -4 to 4
- values: bfloat16 [4096, 512], P(('parts', 'tok')), parts along dimension 0, may hold values from -5 to 5
- outputs: bfloat16 [4096, 4096], P(('parts', 'tok')), parts along dimension 0, may hold values from -3 to 3
- out_grad: bfloat16 [4096, 4096], P(('parts', 'tok')), parts along dimension 0, may hold values from -6 to 6
- ancestors: int32 [32, 10], P('parts'), parts along dimension 0, may hold values from -1 to 14, as said below
Outputs:
- query_grad: bfloat16 [4096, 4096], P(('parts', 'tok')), parts along dimension 0
- key_grad: bfloat16 [4096, 512], P(('parts', 'tok')), parts along dimension 0
- value_grad: bfloat16 [4096, 512], P(('parts', 'tok')), parts along dimension 0
The draws below stay inside these ranges and needn't reach their ends.
There are 2 independent parts, one for each index of `parts`. The reference program is written for one: setup_inputs(seed, part) draws one part's arguments, and reference() takes and returns one part's arrays. A program takes and returns all parts, laid end to end along the dimension named above; each array names one. Nothing has to cross between parts.
Inputs may be any that keep to these rules, and one draw needn't show every extreme that they name: Row t lists the ancestor tiles of tile t, from its parent up to tile 0, each once, then -1 to the end. Every listed tile is earlier than t; tile 0 is an ancestor of every other tile and has none; some tile has exactly 10 ancestors.
All inputs are finite; a program needn't handle non-finite values.
Results may differ from the reference program's by a relative error of at most 0.0053.
Values may be sent and summed in bfloat16 or wider, within the bound.
A program may use at most 128 MiB of HBM per device.

```python
import jax
import jax.numpy as jnp
from jax import lax

QH = 32
KVH = 4
HD = 128
TILE = 128
NT = 16
TOKENS = 2048
DEPTH = 10


def draw_queries(key, part):
    result = jnp.clip(jax.random.normal(jax.random.fold_in(key, 1), (TOKENS, QH, HD), jnp.float32), -4.0, 4.0)
    return result.reshape(TOKENS, QH * HD).astype(jnp.bfloat16)


def draw_keys(key, part):
    result = jnp.clip(jax.random.normal(jax.random.fold_in(key, 2), (TOKENS, KVH, HD), jnp.float32), -4.0, 4.0)
    return result.reshape(TOKENS, KVH * HD).astype(jnp.bfloat16)


def draw_ancestors(key, part):
    base_key = jax.random.fold_in(key, 23)
    chain_key, coin_key, pick_key = jax.random.split(base_key, 3)
    ranking = jnp.argsort(jax.random.randint(chain_key, (NT - 1,), 0, 1 << 30), stable=True).astype(jnp.int32) + 1
    chain = jnp.sort(ranking[:DEPTH]).astype(jnp.int32)
    in_chain = jnp.zeros((NT,), jnp.bool_).at[chain].set(True)
    chain_parent = jnp.zeros((NT,), jnp.int32).at[chain].set(jnp.concatenate([jnp.zeros((1,), jnp.int32), chain[:-1]]))
    coins = jax.random.randint(coin_key, (NT,), 0, 2)
    picks = jax.random.randint(pick_key, (NT,), 0, 1 << 30)

    def place(index, state):
        parents, depths = state
        guess = jnp.where(coins[index] == 1, index - 1, picks[index] % index).astype(jnp.int32)
        guess = jnp.where(depths[guess] >= DEPTH, parents[guess], guess)
        chosen_parent = jnp.where(in_chain[index], chain_parent[index], guess)
        return (parents.at[index].set(chosen_parent), depths.at[index].set(depths[chosen_parent] + 1))
    parents, depths = lax.fori_loop(1, NT, place, (jnp.full((NT,), -1, jnp.int32), jnp.zeros((NT,), jnp.int32)))
    columns = []
    current = parents
    for level in range(DEPTH):
        columns.append(current)
        current = jnp.where(current >= 0, parents[jnp.maximum(current, 0)], -1).astype(jnp.int32)
    return jnp.stack(columns, axis=1).astype(jnp.int32)


def levels(key, extent, cuts, low, largest):
    loudness, own = 1.0, jax.random.fold_in(key, 6)
    for dim, blocks in cuts:
        heights = jnp.exp(jax.random.uniform(jax.random.fold_in(own, dim), (blocks,), jnp.float32, low / len(cuts), largest / len(cuts)))
        loudness = loudness * jnp.repeat(heights, extent[dim] // blocks).reshape([-1 if axis == dim else 1 for axis in range(len(extent))])
    return loudness


def gaussian(stream_key, extent, spread, most, cuts=(), kind=jnp.bfloat16):
    values = spread * jax.random.normal(stream_key, extent, jnp.float32)
    if cuts:
        values = values * levels(stream_key, extent, cuts, -0.22, 0.18)
    return jnp.clip(values, -most, most).astype(kind)


def setup_inputs(seed: int = 0, part: int = 0) -> dict:
    key_of = jax.random.split(jax.random.key(seed), 7)
    part_splits = jax.random.split(jax.random.fold_in(key_of[6], part), 7)
    return {
        "queries": draw_queries(jax.random.fold_in(jax.random.fold_in(key_of[6], part), 71), part),
        "keys": draw_keys(jax.random.fold_in(jax.random.fold_in(key_of[6], part), 71), part),
        "values": gaussian(part_splits[2], (TOKENS, KVH * HD), 1.0, 5.0, ((0, 16),)),
        "outputs": gaussian(part_splits[3], (TOKENS, QH * HD), 0.5, 3.0, ((0, 16),)),
        "out_grad": gaussian(part_splits[4], (TOKENS, QH * HD), 1.0, 6.0, ((0, 16),)),
        "ancestors": draw_ancestors(jax.random.fold_in(jax.random.fold_in(key_of[6], part), 71), part),
    }


def reference(queries, keys, values, outputs, out_grad, ancestors):
    tile_count = ancestors.shape[0]
    slot_count = ancestors.shape[1] + 1
    groups = QH // KVH
    softmax_scale = HD ** -0.5
    query_tiles = queries.reshape(tile_count, TILE, KVH, groups, HD)
    output_tiles = outputs.reshape(tile_count, TILE, KVH, groups, HD)
    grad_tiles = out_grad.reshape(tile_count, TILE, KVH, groups, HD)
    key_tiles = keys.reshape(tile_count, TILE, KVH, HD)
    value_tiles = values.reshape(tile_count, TILE, KVH, HD)
    own_tiles = jnp.arange(tile_count, dtype=jnp.int32)[:, None]
    key_lists = jnp.concatenate([ancestors.astype(jnp.int32), own_tiles], axis=1)
    causal = jnp.arange(TILE)[:, None] >= jnp.arange(TILE)[None, :]
    not_self = jnp.arange(slot_count) != slot_count - 1

    def scan_step(carry, tile_index):
        key_acc, value_acc = carry
        tile_row = key_lists[tile_index]
        is_live = tile_row >= 0
        safe_tiles = jnp.maximum(tile_row, 0).astype(jnp.int32)
        key_block = key_tiles[safe_tiles].astype(jnp.float32)
        value_block = value_tiles[safe_tiles].astype(jnp.float32)
        query_block = query_tiles[tile_index].astype(jnp.float32)
        output_block = output_tiles[tile_index].astype(jnp.float32)
        grad_block = grad_tiles[tile_index].astype(jnp.float32)
        scores = jnp.einsum("ikgd,sjkd->kgisj", query_block, key_block) * softmax_scale
        key_mask = is_live[None, :, None] & (not_self[None, :, None] | causal[:, None, :])
        scores = jnp.where(key_mask, scores, -jnp.inf)
        row_max = jnp.max(scores, axis=(3, 4), keepdims=True)
        log_total = row_max + jnp.log(jnp.sum(jnp.exp(scores - row_max), axis=(3, 4), keepdims=True))
        attn_probs = jnp.exp(scores - log_total)
        probs_low = lax.optimization_barrier(attn_probs.astype(jnp.bfloat16)).astype(jnp.float32)
        grad_probs = jnp.einsum("ikgd,sjkd->kgisj", grad_block, value_block)
        row_delta = jnp.transpose(jnp.sum(grad_block * output_block, axis=-1), (1, 2, 0))[..., None, None]
        grad_scores = lax.optimization_barrier((attn_probs * (grad_probs - row_delta)).astype(jnp.bfloat16)).astype(jnp.float32)
        query_grad = (jnp.einsum("kgisj,sjkd->ikgd", grad_scores, key_block) * softmax_scale).astype(jnp.bfloat16)
        key_part = jnp.einsum("kgisj,ikgd->sjkd", grad_scores, query_block)
        value_part = jnp.einsum("kgisj,ikgd->sjkd", probs_low, grad_block)
        keep_mask = is_live[:, None, None, None]
        key_acc = key_acc.at[safe_tiles].add(jnp.where(keep_mask, key_part, 0.0))
        value_acc = value_acc.at[safe_tiles].add(jnp.where(keep_mask, value_part, 0.0))
        return (key_acc, value_acc), query_grad

    zeros_acc = jnp.zeros((tile_count, TILE, KVH, HD), jnp.float32)
    (key_acc, value_acc), query_grad = lax.scan(scan_step, (zeros_acc, zeros_acc), jnp.arange(tile_count, dtype=jnp.int32))
    token_count = tile_count * TILE
    key_grad = (key_acc * softmax_scale).astype(jnp.bfloat16).reshape(token_count, KVH * HD)
    value_grad = value_acc.astype(jnp.bfloat16).reshape(token_count, KVH * HD)
    return (query_grad.reshape(token_count, QH * HD), key_grad, value_grad)
```

```python
import functools
import math

import jax
import jax.numpy as jnp
from jax import lax
from jax.experimental import pallas as pl
from jax.experimental.pallas import tpu as pltpu
from jax.sharding import PartitionSpec as P

QH = 32
KVH = 4
HD = 128
TILE = 128
GROUP = QH // KVH
ROWS = GROUP * TILE
SCALE = HD ** -0.5
EXP_SCALE = SCALE * math.log2(math.e)
LOOP = lax.fori_loop
NY = 2
NC = 2
MINE = KVH // NC
STAGES = 2 * MINE
UNROLL = 6


class Place:
    def __init__(self, tiles):
        self.nz = tiles // (NY * NC)
        tok = lax.axis_index("tok")
        self.z = tok // (NY * NC)
        self.y = lax.rem(tok // NC, NY)
        self.c = lax.rem(tok, NC)
        self.below_top = self.z + 1 < self.nz

    def tile(self, z, y, c):
        return (z * NY + y) * NC + c

    def chip(self, z, y):
        return pl.ds((z * NY + y) * NC, NC)

    def at(self, z, y, c):
        z = jnp.clip(z, 0, self.nz - 1)
        return {"tok": self.tile(z, y, c)}

    def meet(self):
        barrier = pltpu.get_barrier_semaphore()

        def greet(z, y, c):
            pl.semaphore_signal(barrier, 1, device_id=self.at(z, y, c))

        for c in range(NC):
            for d in (1, 2):
                pl.when(self.z >= d)(lambda d=d, c=c: greet(self.z - d, self.y, c))
                pl.when(self.z + d < self.nz)(lambda d=d, c=c: greet(self.z + d, self.y, c))
            greet(self.z, 1 - self.y, c)
        greet(self.z, self.y, 1 - self.c)
        reach = jnp.minimum(self.z, 2) + jnp.minimum(self.nz - 1 - self.z, 2) + 1
        pl.semaphore_wait(barrier, NC * reach + 1)


def each(start, stop, body):
    def step(i, carry):
        body(i)
        return carry

    LOOP(start, stop, step, 0)


class Gather:
    def __init__(self, place, own, buf, sems):
        self.p, self.own_refs, self.buf = place, own, buf
        self.os, self.rs, self.us, self.ur, self.zs, self.zr, self.ys, self.yr = sems

    @staticmethod
    def sems(nz):
        dma = pltpu.SemaphoreType.DMA
        return [
            dma((STAGES, NC, 4)), dma((STAGES, 4, NC)), dma((STAGES,)), dma((STAGES,)),
            dma((STAGES, nz)), dma((STAGES, nz)), dma((STAGES, nz)), dma((STAGES, nz)),
        ]

    def small(self, q, lane, route):
        p = self.p
        kind, i = q // MINE, q % MINE
        columns = pl.ds(pl.multiple_of((lane * MINE + i) * HD, HD), HD)
        target = (
            p.at(p.z, p.y, lane), p.at(p.z, 1 - p.y, lane), p.at(p.z + 1, p.y, lane), p.at(p.z + 2, p.y, lane),
        )[route]
        return pltpu.make_async_remote_copy(
            self.own_refs[kind].at[:, columns], self.buf[q].at[p.tile(p.z, p.y, p.c)],
            self.os.at[q, lane, route], self.rs.at[q, route, p.c], device_id=target)

    def got_small(self, q, route, c):
        p = self.p
        z, y = ((p.z, p.y), (p.z, 1 - p.y), (p.z - 1, p.y), (p.z - 2, p.y))[route]
        block = self.buf[q].at[p.tile(jnp.maximum(z, 0), y, c)]
        pltpu.make_async_remote_copy(
            block, block, self.us.at[q], self.rs.at[q, route, c], device_id=p.at(p.z, p.y, 1 - p.c)).wait_recv()

    def up_other(self, q, z):
        p = self.p
        block = self.buf[q].at[p.chip(z, 1 - p.y)]
        return pltpu.make_async_remote_copy(
            block, block, self.us.at[q], self.ur.at[q], device_id=p.at(z + 1, p.y, p.c))

    def up(self, q, z):
        p = self.p
        block = self.buf[q].at[p.chip(z, p.y)]
        return pltpu.make_async_remote_copy(
            block, block, self.zs.at[q, z], self.zr.at[q, z], device_id=p.at(p.z + 1, p.y, p.c))

    def across(self, q, z, y):
        p = self.p
        block = self.buf[q].at[p.chip(z, y)]
        return pltpu.make_async_remote_copy(
            block, block, self.ys.at[q, z], self.yr.at[q, z], device_id=p.at(p.z, 1 - p.y, p.c))

    def routes(self, q, act):
        p = self.p
        for lane in range(NC):
            pl.when(p.below_top)(lambda lane=lane: act(self.small(q, lane, 2)))
        for lane in range(NC):
            pl.when((p.y == 0) | p.below_top)(lambda lane=lane: act(self.small(q, lane, 1)))
            pl.when(p.c != lane)(lambda lane=lane: act(self.small(q, lane, 0)))
        for lane in range(NC):
            pl.when(p.z + 2 < p.nz)(lambda lane=lane: act(self.small(q, lane, 3)))

    def own(self, q):
        self.routes(q, lambda copy: copy.start())

    def peer(self, q):
        p = self.p

        @pl.when((p.y == 1) | p.below_top)
        def _():
            for c in range(NC):
                self.got_small(q, 1, c)

        pl.when(p.below_top)(lambda: self.up_other(q, p.z).start())

    def natives(self, q):
        p = self.p

        def pass_on(z):
            pl.when(p.below_top)(lambda: self.up(q, z).start())
            self.across(q, z, p.y).start()

        @pl.when(p.z >= 2)
        def _():
            for c in range(NC):
                self.got_small(q, 3, c)
            pass_on(p.z - 2)

        def step(i):
            z = p.z - 3 - i
            self.up(q, z).wait_recv()
            pass_on(z)

        each(0, p.z - 2, step)

    def ready(self, q):
        p = self.p
        self.got_small(q, 0, 1 - p.c)

        @pl.when(p.z >= 1)
        def _():
            for c in range(NC):
                self.got_small(q, 2, c)
            self.up_other(q, p.z - 1).wait_recv()

        each(0, p.z - 1, lambda z: self.across(q, z, 1 - p.y).wait_recv())

    def drain(self, q):
        p = self.p
        self.routes(q, lambda copy: copy.wait_send())

        @pl.when(p.below_top)
        def _():
            self.up_other(q, p.z).wait_send()
            each(0, p.z - 1, lambda z: self.up(q, z).wait_send())

        each(0, p.z - 1, lambda z: self.across(q, z, p.y).wait_send())


class Reduce:
    def __init__(self, place, part, slot_of, out, scratch):
        self.p, self.part, self.slot_of, self.out = place, part, slot_of, out
        (self.kept, self.kept_peer, self.total, self.for_y, self.from_y, self.for_z, self.from_z, self.for_other,
         self.from_other, self.ys, self.yr, self.zs, self.zr, self.us, self.ur, self.cs, self.cr) = scratch

    @staticmethod
    def scratch(nz):
        dma = pltpu.SemaphoreType.DMA
        block = (NC, TILE, HD)
        f32, bf16 = jnp.float32, jnp.bfloat16
        return [
            pltpu.VMEM((STAGES, nz) + block, f32),
            pltpu.VMEM((STAGES,) + block, f32),
            pltpu.VMEM((STAGES,) + block, bf16),
            pltpu.VMEM((STAGES, nz) + block, bf16),
            pltpu.VMEM((STAGES, nz) + block, bf16),
            pltpu.VMEM((STAGES, nz) + block, bf16),
            pltpu.VMEM((STAGES, nz + 1) + block, bf16),
            pltpu.VMEM((STAGES,) + block, bf16),
            pltpu.VMEM((STAGES,) + block, bf16),
        ] + [dma((STAGES, nz))] * 3 + [dma((STAGES, nz + 1))] + [dma((STAGES,))] * 4

    def to_y(self, r, z):
        p = self.p
        return pltpu.make_async_remote_copy(
            self.for_y.at[r, z], self.from_y.at[r, z], self.ys.at[r, z], self.yr.at[r, z],
            device_id=p.at(p.z, 1 - p.y, p.c))

    def down(self, r, z, slot, d):
        p = self.p
        return pltpu.make_async_remote_copy(
            self.for_z.at[r, z], self.from_z.at[r, slot], self.zs.at[r, z], self.zr.at[r, slot],
            device_id=p.at(p.z - d, p.y, p.c))

    def down_other(self, r):
        p = self.p
        return pltpu.make_async_remote_copy(
            self.for_other.at[r], self.from_other.at[r], self.us.at[r], self.ur.at[r],
            device_id=p.at(p.z - 1, p.y, p.c))

    def hand_over(self, r):
        p = self.p
        block = self.total.at[r, 1 - p.c]
        columns = pl.ds(pl.multiple_of((p.c * MINE + r % MINE) * HD, HD), HD)
        return pltpu.make_async_remote_copy(
            block, self.out[r // MINE].at[:, columns], self.cs.at[r], self.cr.at[r],
            device_id=p.at(p.z, p.y, 1 - p.c))

    def handed(self, r):
        p = self.p
        block = self.total.at[r, p.c]
        columns = pl.ds(pl.multiple_of(((1 - p.c) * MINE + r % MINE) * HD, HD), HD)
        return pltpu.make_async_remote_copy(
            block, self.out[r // MINE].at[:, columns], self.cs.at[r], self.cr.at[r],
            device_id=p.at(p.z, p.y, 1 - p.c))

    def block(self, z, y, c):
        tile = self.p.tile(z, y, c)
        values = 0.0
        for t in range(NC):
            slot = self.slot_of[t, tile]
            mine = self.part[t, jnp.maximum(slot, 0)]
            values = values + jnp.where(slot >= 0, mine, jnp.zeros_like(mine))
        return values

    def first(self, r):
        p = self.p

        @pl.when(p.z >= 1)
        def _():
            for c in range(NC):
                self.for_other[r, c] = self.block(p.z - 1, 1 - p.y, c).astype(jnp.bfloat16)
            self.down_other(r).start()

        def cross(z):
            for c in range(NC):
                self.for_y[r, z, c] = self.block(z, 1 - p.y, c).astype(jnp.bfloat16)
            self.to_y(r, z).start()

        each(0, p.z - 1, cross)

        @pl.when(p.z >= 1)
        def _():
            for c in range(NC):
                self.for_z[r, p.z - 1, c] = self.block(p.z - 1, p.y, c).astype(jnp.bfloat16)
            self.down(r, p.z - 1, p.nz, 1).start()

        def keep(z):
            for c in range(NC):
                self.kept[r, z, c] = self.block(z, p.y, c)

        each(0, p.z - 1, keep)
        keep(p.z)

        @pl.when(p.y == 1)
        def _():
            for c in range(NC):
                self.kept_peer[r, c] = self.block(p.z, 0, c)

        @pl.when(p.y == 0)
        def _():
            self.kept_peer[r] = jnp.zeros(self.kept_peer.shape[1:], jnp.float32)

    def second(self, r):
        p = self.p

        @pl.when(p.below_top)
        def _():
            self.down_other(r).wait_recv()
            self.for_y[r, p.z] = (self.kept_peer[r] + self.from_other[r].astype(jnp.float32)).astype(jnp.bfloat16)
            self.to_y(r, p.z).start()

        @pl.when(jnp.logical_not(p.below_top) & (p.y == 1))
        def _():
            self.for_y[r, p.z] = self.kept_peer[r].astype(jnp.bfloat16)
            self.to_y(r, p.z).start()

    def third(self, r):
        p = self.p

        def step(z):
            self.to_y(r, z).wait_recv()

            @pl.when(jnp.logical_not(p.below_top))
            def _():
                self.for_z[r, z] = (self.kept[r, z] + self.from_y[r, z].astype(jnp.float32)).astype(jnp.bfloat16)

            @pl.when(p.below_top)
            def _():
                self.down(r, z, z, 1).wait_recv()
                total = self.kept[r, z] + self.from_y[r, z].astype(jnp.float32)
                self.for_z[r, z] = (total + self.from_z[r, z].astype(jnp.float32)).astype(jnp.bfloat16)

            pl.when(z == p.z - 2)(lambda: self.down(r, z, p.z, 2).start())
            pl.when(z < p.z - 2)(lambda: self.down(r, z, z, 1).start())

        each(0, p.z - 1, step)

    def fourth(self, r):
        p = self.p

        @pl.when((p.y == 0) | p.below_top)
        def _():
            self.to_y(r, p.z).wait_recv()
            self.kept[r, p.z] += self.from_y[r, p.z].astype(jnp.float32)

        @pl.when(p.below_top)
        def _():
            self.down(r, p.z, p.nz, 1).wait_recv()
            self.kept[r, p.z] += self.from_z[r, p.nz].astype(jnp.float32)

        @pl.when(p.z + 2 < p.nz)
        def _():
            self.down(r, p.z, p.z + 2, 1).wait_recv()
            self.kept[r, p.z] += self.from_z[r, p.z + 2].astype(jnp.float32)

        self.total[r] = self.kept[r, p.z].astype(jnp.bfloat16)
        self.hand_over(r).start()
        columns = pl.ds(pl.multiple_of((p.c * MINE + r % MINE) * HD, HD), HD)
        self.out[r // MINE][:, columns] = self.total[r, p.c]

    def drain(self, r):
        p = self.p
        self.handed(r).wait_recv()
        self.hand_over(r).wait_send()
        each(0, p.z - 1, lambda z: self.to_y(r, z).wait_send())
        pl.when((p.y == 1) | p.below_top)(lambda: self.to_y(r, p.z).wait_send())
        each(0, p.z, lambda z: self.down(r, z, z, 1).wait_send())
        pl.when(p.z >= 1)(lambda: self.down_other(r).wait_send())


def dot(a, b):
    return jnp.dot(a, b, preferred_element_type=jnp.float32)


def dot_last(a, b):
    return lax.dot_general(
        a, b, (((1,), (1,)), ((), ())), preferred_element_type=jnp.float32)


def fold(x, op):
    return op(x.reshape(TILE // 8, 8, x.shape[-1]), axis=0)


HALVES = (slice(0, TILE), slice(TILE, 2 * TILE))


def backward_kernel(
    tiles, pairs, wide, anc, k_ref, v_ref, q_hbm, g_hbm, o_hbm, dq_hbm, dk_ref, dv_ref,
    slot_of, q_in, g_in, o_in, load_sem, send_sem, recv_sem, store_sem, give_sem, take_sem,
    qs, gs, delta, scores, peak, total, inverse, dqt, part, *rest,
):
    place = Place(tiles)
    z, y, c = place.z, place.y, place.c
    depth = anc.shape[1]
    buf, rest = rest[:STAGES], rest[STAGES:]
    gather = Gather(place, (k_ref, v_ref), buf, rest[:8])
    reduce = Reduce(place, part, slot_of, (dv_ref, dk_ref), rest[8:])
    arrays = ((q_hbm, q_in), (g_hbm, g_in), (o_hbm, o_in))

    def slab(core, i):
        return pl.ds(pl.multiple_of((core * MINE + i) * ROWS, ROWS), ROWS)

    def load(i, which):
        src, dst = arrays[which]
        return pltpu.make_async_copy(src.at[:, slab(c, i)], dst.at[c, i], load_sem.at[i, which])

    def lend(i, which):
        src, dst = arrays[which]
        return pltpu.make_async_remote_copy(
            src.at[:, slab(1 - c, i)], dst.at[c, i], send_sem.at[i, which], recv_sem.at[i, which],
            device_id=place.at(z, y, 1 - c))

    def borrowed(i, which):
        src, dst = arrays[which]
        return pltpu.make_async_remote_copy(
            src.at[:, slab(c, i)], dst.at[1 - c, i], send_sem.at[i, which], recv_sem.at[i, which],
            device_id=place.at(z, y, 1 - c))

    def keep_dq(i):
        return pltpu.make_async_copy(q_in.at[c, i], dq_hbm.at[:, slab(c, i)], store_sem.at[i])

    def give_dq(i):
        return pltpu.make_async_remote_copy(
            q_in.at[1 - c, i], dq_hbm.at[:, slab(c, i)], give_sem.at[i], take_sem.at[i],
            device_id=place.at(z, y, 1 - c))

    def take_dq(i):
        return pltpu.make_async_remote_copy(
            q_in.at[1 - c, i], dq_hbm.at[:, slab(1 - c, i)], give_sem.at[i], take_sem.at[i],
            device_id=place.at(z, y, 1 - c))

    def each_array(i, act):
        for which in range(3):
            act(i, which)

    def me(t):
        return place.tile(z, y, t)

    def over_pairs(body):
        if wide:
            for i in range(pairs):
                body(i)
        else:
            each(0, pairs, body)

    def listed(t, i):
        return jnp.where(i < depth, anc[me(t), jnp.minimum(i, depth - 1)], -1)

    def find(tile):
        for t in range(NC):
            slot = jnp.where(tile == me(t), 0, -1)
            for i in range(depth):
                slot = jnp.where(listed(t, i) == tile, i + 1, slot)
            slot_of[t, tile] = slot

    def stack(i):
        each_array(i, lambda i, which: load(i, which).wait())
        each_array(i, lambda i, which: borrowed(i, which).wait_recv())

        def step(h):
            rows = pl.ds(pl.multiple_of(h * TILE, TILE), TILE)
            for t in range(NC):
                q, go = q_in[t, i, :, rows], g_in[t, i, :, rows]
                qs[t, i, rows, :] = q
                gs[t, i, rows, :] = go
                product = go.astype(jnp.float32) * o_in[t, i, :, rows].astype(jnp.float32)
                delta[t, i, :, rows] = jnp.sum(product.T, axis=0, keepdims=True)

        each(0, GROUP, step)

    def place_of(i, t):
        return i * NC + t if wide else t

    def key_tile(i, t):
        return buf[i][me(t)]

    def tile_pair(q, t, n):
        return jnp.concatenate([buf[q][jnp.maximum(listed(t, 2 * n + j), 0)] for j in range(2)], axis=0)

    def score(i, t):
        b = place_of(i, t)
        buf[i][me(c)] = k_ref[:, pl.ds(pl.multiple_of((c * MINE + i) * HD, HD), HD)]
        s = dot_last(key_tile(i, t), qs[t, i])
        key_pos = lax.broadcasted_iota(jnp.int32, s.shape, 0)
        query_pos = lax.broadcasted_iota(jnp.int32, s.shape, 1) & (TILE - 1)
        s = jnp.where(key_pos <= query_pos, s, -1e30)
        scores[b, 0] = s
        peak[t] = fold(s, jnp.max)

        def step(n):
            s = dot_last(tile_pair(i, t, n), qs[t, i])
            for j, half in enumerate(HALVES):
                scores[b, 1 + 2 * n + j] = s[half]
                bias = jnp.where(listed(t, 2 * n + j) >= 0, 0.0, -1e30)
                peak[t] = jnp.maximum(peak[t], fold(s[half], jnp.max) + bias)

        over_pairs(step)

    def weigh(i, t):
        b = place_of(i, t)
        top = jnp.max(peak[t], axis=0, keepdims=True)
        w = jnp.exp2((scores[b, 0] - top) * EXP_SCALE)
        scores[b, 0] = w
        total[t] = fold(w, jnp.sum)

        def step(n):
            for j in range(2):
                slot = 1 + 2 * n + j
                top_here = top + jnp.where(listed(t, 2 * n + j) >= 0, 0.0, 1e30)
                w = jnp.exp2((scores[b, slot] - top_here) * EXP_SCALE)
                scores[b, slot] = w
                total[t] += fold(w, jnp.sum)

        over_pairs(step)
        inverse[b] = 1.0 / jnp.sum(total[t], axis=0, keepdims=True)

    def value_part(i, t):
        b = place_of(i, t)
        part[t, 0] = dot((scores[b, 0] * inverse[b]).astype(jnp.bfloat16), gs[t, i])

        def step(n):
            first = 1 + 2 * n
            p = scores[b, pl.ds(first, 2)].reshape(2 * TILE, ROWS) * inverse[b]
            dv = dot(p.astype(jnp.bfloat16), gs[t, i])
            for j, half in enumerate(HALVES):
                part[t, first + j] = dv[half]

        over_pairs(step)

    def key_part(i, t):
        b = place_of(i, t)
        q = MINE + i
        buf[q][me(c)] = v_ref[:, pl.ds(pl.multiple_of((c * MINE + i) * HD, HD), HD)]
        slope = dot_last(buf[q][me(t)], gs[t, i]) - delta[t, i]
        ds = (scores[b, 0] * inverse[b] * slope).astype(jnp.bfloat16)
        part[t, 0] = dot(ds, qs[t, i]) * SCALE
        dqt[...] = dot(key_tile(i, t).T, ds)

        def step(n):
            first = 1 + 2 * n
            slope = dot_last(tile_pair(q, t, n), gs[t, i]) - delta[t, i]
            p = scores[b, pl.ds(first, 2)].reshape(2 * TILE, ROWS) * inverse[b]
            ds = (p * slope).astype(jnp.bfloat16)
            dk = dot(ds, qs[t, i]) * SCALE
            for j, half in enumerate(HALVES):
                part[t, first + j] = dk[half]
            dqt[...] += dot(tile_pair(i, t, n).T, ds)

        over_pairs(step)
        for h in range(GROUP):
            rows = slice(h * TILE, (h + 1) * TILE)
            q_in[t, i, :, rows] = (dqt[:, rows].T * SCALE).astype(jnp.bfloat16)

    each_array(0, lambda i, which: load(i, which).start())
    each_array(1, lambda i, which: load(i, which).start())
    place.meet()

    def finish_query(i):
        keep_dq(i).start()
        give_dq(i).start()

    if wide:
        gather.own(0)
        each_array(0, lambda i, which: lend(i, which).start())
        gather.own(1)
        gather.peer(0)
        each(0, tiles, find)
        stack(0)
        gather.natives(0)
        gather.own(2)
        gather.peer(1)
        each_array(1, lambda i, which: lend(i, which).start())
        gather.ready(0)
        score(0, 0)
        gather.natives(1)
        score(0, 1)
        gather.own(3)
        gather.peer(2)
        for t in range(NC):
            weigh(0, t)
            value_part(0, t)
        reduce.first(0)
        stack(1)
        gather.natives(2)
        gather.peer(3)
        gather.ready(1)
        score(1, 0)
        score(1, 1)
        reduce.second(0)
        weigh(1, 0)
        value_part(1, 0)
        reduce.third(0)
        weigh(1, 1)
        value_part(1, 1)
        reduce.first(1)
        gather.natives(3)
        gather.ready(2)
        key_part(0, 0)
        reduce.second(1)
        key_part(0, 1)
        finish_query(0)
        reduce.first(2)
        reduce.third(1)
        gather.ready(3)
        key_part(1, 0)
        reduce.second(2)
        reduce.third(2)
        key_part(1, 1)
        finish_query(1)
        reduce.first(3)
        reduce.second(3)
        reduce.third(3)
    else:
        each(0, tiles, find)
        for i in range(MINE):
            each_array(i, lambda i, which: lend(i, which).start())
            for q in (i, MINE + i):
                gather.own(q)
                gather.peer(q)
                gather.natives(q)
                gather.ready(q)
            stack(i)
            for t in range(NC):
                score(i, t)
                weigh(i, t)
                value_part(i, t)
            reduce.first(i)
            for t in range(NC):
                key_part(i, t)
            finish_query(i)
            reduce.first(MINE + i)
            for r in (i, MINE + i):
                reduce.second(r)
                reduce.third(r)
    for r in range(STAGES):
        reduce.fourth(r)
    for i in range(MINE):
        keep_dq(i).wait()
        give_dq(i).wait_send()
        take_dq(i).wait_recv()
        each_array(i, lambda i, which: lend(i, which).wait_send())
    for r in range(STAGES):
        gather.drain(r)
        reduce.drain(r)


def finish_kernel(a_ref, b_ref, c_ref, x_ref, y_ref, z_ref):
    x_ref[...] = a_ref[...]
    y_ref[...] = b_ref[...]
    z_ref[...] = c_ref[...]


def per_device(tiles, queries, keys, values, outputs, out_grad, ancestors):
    depth = ancestors.shape[1]
    pairs = (depth + 1) // 2
    slots = 1 + 2 * pairs
    nz = tiles // (NY * NC)
    wide = pairs <= UNROLL
    vmem = pl.BlockSpec(memory_space=pltpu.VMEM)
    smem = pl.BlockSpec(memory_space=pltpu.SMEM)
    hbm = pl.BlockSpec(memory_space=pl.ANY)
    f32, bf16 = jnp.float32, jnp.bfloat16
    dma = pltpu.SemaphoreType.DMA
    shapes = (
        jax.ShapeDtypeStruct(queries.shape, bf16),
        jax.ShapeDtypeStruct(keys.shape, bf16),
        jax.ShapeDtypeStruct(values.shape, bf16),
    )
    results = pl.pallas_call(
        functools.partial(backward_kernel, tiles, pairs, wide),
        out_shape=shapes,
        in_specs=[smem] + [vmem] * 2 + [hbm] * 3,
        out_specs=(hbm, vmem, vmem),
        scratch_shapes=[
            pltpu.SMEM((NC, tiles), jnp.int32),
            pltpu.VMEM((NC, MINE, TILE, ROWS), bf16),
            pltpu.VMEM((NC, MINE, TILE, ROWS), bf16),
            pltpu.VMEM((NC, MINE, TILE, ROWS), bf16),
            dma((MINE, 3)), dma((MINE, 3)), dma((MINE, 3)), dma((MINE,)), dma((MINE,)), dma((MINE,)),
            pltpu.VMEM((NC, MINE, ROWS, HD), bf16),
            pltpu.VMEM((NC, MINE, ROWS, HD), bf16),
            pltpu.VMEM((NC, MINE, 1, ROWS), f32),
            pltpu.VMEM((NC * MINE if wide else NC, slots, TILE, ROWS), f32),
            pltpu.VMEM((NC, 8, ROWS), f32),
            pltpu.VMEM((NC, 8, ROWS), f32),
            pltpu.VMEM((NC * MINE, 1, ROWS), f32),
            pltpu.VMEM((HD, ROWS), f32),
            pltpu.VMEM((NC, slots, TILE, HD), f32),
        ]
        + [pltpu.VMEM((tiles, TILE, HD), bf16)] * STAGES
        + Gather.sems(nz)
        + Reduce.scratch(nz),
        compiler_params=pltpu.CompilerParams(
            collective_id=0, has_side_effects=True, vmem_limit_bytes=62 << 20),
    )(ancestors, keys, values, queries, out_grad, outputs)
    steps = 4

    def columns(shape):
        return pl.BlockSpec((shape.shape[0], shape.shape[1] // steps), lambda i: (0, i))

    specs = tuple(columns(shape) for shape in shapes)
    return pl.pallas_call(
        finish_kernel, out_shape=shapes, grid=(steps,), in_specs=list(specs), out_specs=specs,
    )(*results)


def solution(mesh):
    rows = P(("parts", "tok"), None)
    return jax.shard_map(
        functools.partial(per_device, mesh.shape["tok"]),
        mesh=mesh,
        in_specs=(rows,) * 5 + (P("parts", None),),
        out_specs=(rows,) * 3,
        check_vma=False,
    )
```

```python
import functools
import math

import jax
import jax.numpy as jnp
from jax import lax
from jax.experimental import pallas as pl
from jax.experimental.pallas import tpu as pltpu
from jax.sharding import PartitionSpec as P

QH = 32
KVH = 4
HD = 128
TILE = 128
GROUP = QH // KVH
ROWS = GROUP * TILE
SCALE = HD ** -0.5
EXP_SCALE = SCALE * math.log2(math.e)
LOOP = lax.fori_loop
NY = 2
NC = 2
MINE = KVH // NC
STAGES = 2 * MINE
UNROLL = 6


class Place:
    def __init__(self, tiles):
        self.nz = tiles // (NY * NC)
        tok = lax.axis_index("tok")
        self.z = tok // (NY * NC)
        self.y = lax.rem(tok // NC, NY)
        self.c = lax.rem(tok, NC)
        self.below_top = self.z + 1 < self.nz
        self.next_to_top = self.z + 2 == self.nz
        self.crossing = jnp.where(self.below_top, self.z, self.z - 1)

    def tile(self, z, y, c):
        return (z * NY + y) * NC + c

    def chip(self, z, y):
        return pl.ds((z * NY + y) * NC, NC)

    def at(self, z, y, c):
        z = jnp.clip(z, 0, self.nz - 1)
        return {"tok": self.tile(z, y, c)}

    def meet(self):
        barrier = pltpu.get_barrier_semaphore()

        def greet(z, y, c):
            pl.semaphore_signal(barrier, 1, device_id=self.at(z, y, c))

        for c in range(NC):
            greet(self.z, 1 - self.y, c)
            for d in range(1, self.nz):
                greet(lax.rem(self.z + d, self.nz), self.y, c)
        greet(self.z, self.y, 1 - self.c)
        pl.semaphore_wait(barrier, NC * self.nz + 1)


def each(start, stop, body):
    def step(i, carry):
        body(i)
        return carry

    LOOP(start, stop, step, 0)


class Gather:
    def __init__(self, place, own, buf, sems):
        self.p, self.own_refs, self.buf = place, own, buf
        self.os, self.rs, self.us, self.ur, self.ys, self.yr = sems

    @staticmethod
    def sems(nz):
        dma = pltpu.SemaphoreType.DMA
        return [
            dma((STAGES, NC, nz + 1)), dma((STAGES, NC, nz + 1)), dma((STAGES,)), dma((STAGES,)),
            dma((STAGES, nz)), dma((STAGES, nz)),
        ]

    def small(self, q, lane, route):
        p = self.p
        kind, i = q // MINE, q % MINE
        columns = pl.ds(pl.multiple_of((lane * MINE + i) * HD, HD), HD)
        target = p.at(p.z + route, p.y, lane) if route < p.nz else p.at(p.z, 1 - p.y, lane)
        return pltpu.make_async_remote_copy(
            self.own_refs[kind].at[:, columns], self.buf[q].at[p.tile(p.z, p.y, p.c)],
            self.os.at[q, lane, route], self.rs.at[q, p.c, route], device_id=target)

    def got_small(self, q, z, y, c, route):
        p = self.p
        block = self.buf[q].at[p.tile(z, y, c)]
        pltpu.make_async_remote_copy(
            block, block, self.us.at[q], self.rs.at[q, c, route], device_id=p.at(p.z, p.y, 1 - p.c)).wait_recv()

    def up_other(self, q, z):
        p = self.p
        block = self.buf[q].at[p.chip(z, 1 - p.y)]
        return pltpu.make_async_remote_copy(
            block, block, self.us.at[q], self.ur.at[q], device_id=p.at(z + 1, p.y, p.c))

    def across(self, q, z, y):
        p = self.p
        block = self.buf[q].at[p.chip(z, y)]
        return pltpu.make_async_remote_copy(
            block, block, self.ys.at[q, z], self.yr.at[q, z], device_id=p.at(p.z, 1 - p.y, p.c))

    def routes(self, q, act):
        p = self.p
        for lane in range(NC):
            pl.when((p.y == 0) | p.next_to_top)(lambda lane=lane: act(self.small(q, lane, p.nz)))
            pl.when(p.c != lane)(lambda lane=lane: act(self.small(q, lane, 0)))
        for d in range(p.nz - 1, 0, -1):
            for lane in range(NC):
                pl.when(p.z + d < p.nz)(lambda lane=lane, d=d: act(self.small(q, lane, d)))

    def own(self, q):
        self.routes(q, lambda copy: copy.start())

    def peer(self, q):
        p = self.p

        @pl.when((p.y == 1) | p.next_to_top)
        def _():
            for c in range(NC):
                self.got_small(q, p.z, 1 - p.y, c, p.nz)

        pl.when(p.next_to_top)(lambda: self.up_other(q, p.z).start())

    def natives(self, q):
        p = self.p

        def step(z):
            for c in range(NC):
                self.got_small(q, z, p.y, c, p.z - z)
            self.across(q, z, p.y).start()

        each(0, p.crossing, step)

    def ready(self, q):
        p = self.p
        self.got_small(q, p.z, p.y, 1 - p.c, 0)

        @pl.when(jnp.logical_not(p.below_top))
        def _():
            for c in range(NC):
                self.got_small(q, p.z - 1, p.y, c, 1)
            self.up_other(q, p.z - 1).wait_recv()

        each(0, p.crossing, lambda z: self.across(q, z, 1 - p.y).wait_recv())

    def drain(self, q):
        p = self.p
        self.routes(q, lambda copy: copy.wait_send())
        pl.when(p.next_to_top)(lambda: self.up_other(q, p.z).wait_send())
        each(0, p.crossing, lambda z: self.across(q, z, p.y).wait_send())


class Reduce:
    def __init__(self, place, part, slot_of, out, scratch):
        self.p, self.part, self.slot_of, self.out = place, part, slot_of, out
        (self.kept, self.total, self.for_y, self.from_y, self.for_z, self.from_z, self.for_other,
         self.from_other, self.ys, self.yr, self.zs, self.zr, self.us, self.ur, self.cs, self.cr) = scratch

    @staticmethod
    def scratch(nz):
        dma = pltpu.SemaphoreType.DMA
        block = (NC, TILE, HD)
        f32, bf16 = jnp.float32, jnp.bfloat16
        return [
            pltpu.VMEM((STAGES,) + block, f32),
            pltpu.VMEM((STAGES,) + block, bf16),
            pltpu.VMEM((STAGES, nz) + block, bf16),
            pltpu.VMEM((STAGES, nz) + block, bf16),
            pltpu.VMEM((STAGES, nz) + block, bf16),
            pltpu.VMEM((STAGES, nz) + block, bf16),
            pltpu.VMEM((STAGES,) + block, bf16),
            pltpu.VMEM((STAGES,) + block, bf16),
        ] + [dma((STAGES, nz))] * 4 + [dma((STAGES,))] * 4

    def to_y(self, r, z):
        p = self.p
        return pltpu.make_async_remote_copy(
            self.for_y.at[r, z], self.from_y.at[r, z], self.ys.at[r, z], self.yr.at[r, z],
            device_id=p.at(p.z, 1 - p.y, p.c))

    def down(self, r, z):
        p = self.p
        return pltpu.make_async_remote_copy(
            self.for_z.at[r, z], self.from_z.at[r, p.z], self.zs.at[r, z], self.zr.at[r, p.z],
            device_id=p.at(z, p.y, p.c))

    def came_down(self, r, z):
        p = self.p
        pltpu.make_async_remote_copy(
            self.for_z.at[r, z], self.from_z.at[r, z], self.zs.at[r, z], self.zr.at[r, z],
            device_id=p.at(z, p.y, p.c)).wait_recv()

    def down_other(self, r):
        p = self.p
        return pltpu.make_async_remote_copy(
            self.for_other.at[r], self.from_other.at[r], self.us.at[r], self.ur.at[r],
            device_id=p.at(p.z - 1, p.y, p.c))

    def hand_over(self, r):
        p = self.p
        block = self.total.at[r, 1 - p.c]
        columns = pl.ds(pl.multiple_of((p.c * MINE + r % MINE) * HD, HD), HD)
        return pltpu.make_async_remote_copy(
            block, self.out[r // MINE].at[:, columns], self.cs.at[r], self.cr.at[r],
            device_id=p.at(p.z, p.y, 1 - p.c))

    def handed(self, r):
        p = self.p
        block = self.total.at[r, p.c]
        columns = pl.ds(pl.multiple_of(((1 - p.c) * MINE + r % MINE) * HD, HD), HD)
        return pltpu.make_async_remote_copy(
            block, self.out[r // MINE].at[:, columns], self.cs.at[r], self.cr.at[r],
            device_id=p.at(p.z, p.y, 1 - p.c))

    def block(self, r, z, y, c):
        tile = self.p.tile(z, y, c)
        values = 0.0
        for t in range(NC):
            slot = self.slot_of[t, tile]
            mine = self.part[r, t, jnp.maximum(slot, 0)]
            values = values + jnp.where(slot >= 0, mine, jnp.zeros_like(mine))
        return values

    def first(self, r):
        p = self.p

        def cross(z):
            for c in range(NC):
                self.for_y[r, z, c] = self.block(r, z, 1 - p.y, c).astype(jnp.bfloat16)
            self.to_y(r, z).start()

        each(0, p.crossing, cross)
        pl.when((p.y == 1) & jnp.logical_not(p.next_to_top))(lambda: cross(p.z))

        @pl.when(jnp.logical_not(p.below_top))
        def _():
            for c in range(NC):
                self.for_other[r, c] = self.block(r, p.z - 1, 1 - p.y, c).astype(jnp.bfloat16)
            self.down_other(r).start()
            for c in range(NC):
                self.for_z[r, p.z - 1, c] = self.block(r, p.z - 1, p.y, c).astype(jnp.bfloat16)
            self.down(r, p.z - 1).start()

    def second(self, r):
        p = self.p

        @pl.when(p.next_to_top)
        def _():
            self.down_other(r).wait_recv()
            for c in range(NC):
                mine = jnp.where(p.y == 1, self.block(r, p.z, 1 - p.y, c), 0.0)
                self.for_y[r, p.z, c] = (mine + self.from_other[r, c].astype(jnp.float32)).astype(jnp.bfloat16)
            self.to_y(r, p.z).start()

    def third(self, r):
        p = self.p

        def step(z):
            self.to_y(r, z).wait_recv()
            for c in range(NC):
                total = self.block(r, z, p.y, c) + self.from_y[r, z, c].astype(jnp.float32)
                self.for_z[r, z, c] = total.astype(jnp.bfloat16)
            self.down(r, z).start()

        each(0, p.crossing, step)

    def fourth(self, r):
        p = self.p
        for c in range(NC):
            self.kept[r, c] = self.block(r, p.z, p.y, c)

        @pl.when((p.y == 0) | p.next_to_top)
        def _():
            self.to_y(r, p.z).wait_recv()
            self.kept[r] += self.from_y[r, p.z].astype(jnp.float32)

        def step(z):
            self.came_down(r, z)
            self.kept[r] += self.from_z[r, z].astype(jnp.float32)

        each(p.z + 1, p.nz, step)
        self.total[r] = self.kept[r].astype(jnp.bfloat16)
        self.hand_over(r).start()
        columns = pl.ds(pl.multiple_of((p.c * MINE + r % MINE) * HD, HD), HD)
        self.out[r // MINE][:, columns] = self.total[r, p.c]

    def drain(self, r):
        p = self.p
        self.handed(r).wait_recv()
        self.hand_over(r).wait_send()
        each(0, p.crossing, lambda z: self.to_y(r, z).wait_send())
        pl.when((p.y == 1) | p.next_to_top)(lambda: self.to_y(r, p.z).wait_send())
        each(0, p.z, lambda z: self.down(r, z).wait_send())
        pl.when(jnp.logical_not(p.below_top))(lambda: self.down_other(r).wait_send())


def dot(a, b):
    return jnp.dot(a, b, preferred_element_type=jnp.float32)


def dot_last(a, b):
    return lax.dot_general(
        a, b, (((1,), (1,)), ((), ())), preferred_element_type=jnp.float32)


def fold(x, op):
    return op(x.reshape(TILE // 8, 8, x.shape[-1]), axis=0)


HALVES = (slice(0, TILE), slice(TILE, 2 * TILE))


def backward_kernel(
    tiles, pairs, wide, anc, k_ref, v_ref, q_hbm, g_hbm, o_hbm, dq_hbm, dk_ref, dv_ref,
    slot_of, q_in, g_in, o_in, load_sem, send_sem, recv_sem, store_sem, give_sem, take_sem,
    qs, gs, delta, scores, slopes, peak, total, inverse, dqt, part, *rest,
):
    place = Place(tiles)
    z, y, c = place.z, place.y, place.c
    depth = anc.shape[1]
    buf, rest = rest[:STAGES], rest[STAGES:]
    gather = Gather(place, (k_ref, v_ref), buf, rest[:6])
    reduce = Reduce(place, part, slot_of, (dv_ref, dk_ref), rest[6:])
    arrays = ((q_hbm, q_in), (g_hbm, g_in), (o_hbm, o_in))

    def slab(core, i):
        return pl.ds(pl.multiple_of((core * MINE + i) * ROWS, ROWS), ROWS)

    def load(i, which):
        src, dst = arrays[which]
        return pltpu.make_async_copy(src.at[:, slab(c, i)], dst.at[c, i], load_sem.at[i, which])

    def lend(i, which):
        src, dst = arrays[which]
        return pltpu.make_async_remote_copy(
            src.at[:, slab(1 - c, i)], dst.at[c, i], send_sem.at[i, which], recv_sem.at[i, which],
            device_id=place.at(z, y, 1 - c))

    def borrowed(i, which):
        src, dst = arrays[which]
        return pltpu.make_async_remote_copy(
            src.at[:, slab(c, i)], dst.at[1 - c, i], send_sem.at[i, which], recv_sem.at[i, which],
            device_id=place.at(z, y, 1 - c))

    def keep_dq(i):
        return pltpu.make_async_copy(q_in.at[c, i], dq_hbm.at[:, slab(c, i)], store_sem.at[i])

    def give_dq(i):
        return pltpu.make_async_remote_copy(
            q_in.at[1 - c, i], dq_hbm.at[:, slab(c, i)], give_sem.at[i], take_sem.at[i],
            device_id=place.at(z, y, 1 - c))

    def take_dq(i):
        return pltpu.make_async_remote_copy(
            q_in.at[1 - c, i], dq_hbm.at[:, slab(1 - c, i)], give_sem.at[i], take_sem.at[i],
            device_id=place.at(z, y, 1 - c))

    def each_array(i, act):
        for which in range(3):
            act(i, which)

    def me(t):
        return place.tile(z, y, t)

    def weave(*works):
        if wide:
            for n in range(-1, pairs):
                for work in works:
                    work(n)
        else:
            for work in works:
                work(-1)
                each(0, pairs, work)

    def listed(t, i):
        return jnp.where(i < depth, anc[me(t), jnp.minimum(i, depth - 1)], -1)

    def find(tile):
        for t in range(NC):
            slot = jnp.where(tile == me(t), 0, -1)
            for i in range(depth):
                slot = jnp.where(listed(t, i) == tile, i + 1, slot)
            slot_of[t, tile] = slot

    def stack(i):
        each_array(i, lambda i, which: load(i, which).wait())
        each_array(i, lambda i, which: borrowed(i, which).wait_recv())

        def step(h):
            rows = pl.ds(pl.multiple_of(h * TILE, TILE), TILE)
            for t in range(NC):
                q, go = q_in[t, i, :, rows], g_in[t, i, :, rows]
                qs[t, i, rows, :] = q
                gs[t, i, rows, :] = go
                product = go.astype(jnp.float32) * o_in[t, i, :, rows].astype(jnp.float32)
                delta[t, i, :, rows] = jnp.sum(product.T, axis=0, keepdims=True)

        each(0, GROUP, step)

    def place_of(i, t):
        return i * NC + t if wide else t

    def key_tile(i, t):
        return buf[i][me(t)]

    def tile_pair(q, t, n):
        return jnp.concatenate([buf[q][jnp.maximum(listed(t, 2 * n + j), 0)] for j in range(2)], axis=0)

    def score(i, t):
        b = place_of(i, t)

        def step(n):
            if isinstance(n, int) and n < 0:
                s = dot_last(key_tile(i, t), qs[t, i])
                key_pos = lax.broadcasted_iota(jnp.int32, s.shape, 0)
                query_pos = lax.broadcasted_iota(jnp.int32, s.shape, 1) & (TILE - 1)
                s = jnp.where(key_pos <= query_pos, s, -1e30)
                scores[b, 0] = s
                peak[t] = fold(s, jnp.max)
                return
            s = dot_last(tile_pair(i, t, n), qs[t, i])
            for j, half in enumerate(HALVES):
                scores[b, 1 + 2 * n + j] = s[half]
                bias = jnp.where(listed(t, 2 * n + j) >= 0, 0.0, -1e30)
                peak[t] = jnp.maximum(peak[t], fold(s[half], jnp.max) + bias)

        return step

    def weigh(i, t):
        b = place_of(i, t)

        def step(n):
            if isinstance(n, int) and n < 0:
                top = jnp.max(peak[t], axis=0, keepdims=True)
                inverse[b] = top
                w = jnp.exp2((scores[b, 0] - top) * EXP_SCALE)
                scores[b, 0] = w
                total[t] = fold(w, jnp.sum)
                return
            for j in range(2):
                slot = 1 + 2 * n + j
                top = inverse[b] + jnp.where(listed(t, 2 * n + j) >= 0, 0.0, 1e30)
                w = jnp.exp2((scores[b, slot] - top) * EXP_SCALE)
                scores[b, slot] = w
                total[t] += fold(w, jnp.sum)

        return step

    def value_part(i, t):
        b = place_of(i, t)

        def step(n):
            if isinstance(n, int) and n < 0:
                inverse[b] = 1.0 / jnp.sum(total[t], axis=0, keepdims=True)
                part[i, t, 0] = dot((scores[b, 0] * inverse[b]).astype(jnp.bfloat16), gs[t, i])
                return
            first = 1 + 2 * n
            p = scores[b, pl.ds(first, 2)].reshape(2 * TILE, ROWS) * inverse[b]
            dv = dot(p.astype(jnp.bfloat16), gs[t, i])
            for j, half in enumerate(HALVES):
                part[i, t, first + j] = dv[half]

        return step

    def key_part(i, t, later=False):
        b = place_of(i, t)
        q = MINE + i

        def step(n):
            if isinstance(n, int) and n < 0:
                slope = dot_last(buf[q][me(t)], gs[t, i]) - delta[t, i]
                ds = (scores[b, 0] * inverse[b] * slope).astype(jnp.bfloat16)
                part[q, t, 0] = dot(ds, qs[t, i]) * SCALE
                if later:
                    slopes[t, 0] = ds
                else:
                    dqt[t] = dot(key_tile(i, t).T, ds)
                return
            first = 1 + 2 * n
            slope = dot_last(tile_pair(q, t, n), gs[t, i]) - delta[t, i]
            p = scores[b, pl.ds(first, 2)].reshape(2 * TILE, ROWS) * inverse[b]
            ds = (p * slope).astype(jnp.bfloat16)
            dk = dot(ds, qs[t, i]) * SCALE
            for j, half in enumerate(HALVES):
                part[q, t, first + j] = dk[half]
                if later:
                    slopes[t, first + j] = ds[half]
            if not later:
                dqt[t] += dot(tile_pair(i, t, n).T, ds)

        return step

    def query_part(i, t):
        def step(n):
            if isinstance(n, int) and n < 0:
                dqt[t] = dot(key_tile(i, t).T, slopes[t, 0])
                return
            ds = slopes[t, pl.ds(1 + 2 * n, 2)].reshape(2 * TILE, ROWS)
            dqt[t] += dot(tile_pair(i, t, n).T, ds)

        return step

    def turn(i, t):
        for h in range(GROUP):
            rows = slice(h * TILE, (h + 1) * TILE)
            q_in[t, i, :, rows] = (dqt[t, :, rows].T * SCALE).astype(jnp.bfloat16)

    each_array(0, lambda i, which: load(i, which).start())
    each_array(1, lambda i, which: load(i, which).start())
    for i in range(MINE):
        columns = pl.ds(pl.multiple_of((c * MINE + i) * HD, HD), HD)
        buf[i][me(c)] = k_ref[:, columns]
        buf[MINE + i][me(c)] = v_ref[:, columns]
    place.meet()

    def finish_query(i):
        keep_dq(i).start()
        give_dq(i).start()

    if wide:
        gather.own(0)
        each_array(0, lambda i, which: lend(i, which).start())
        gather.own(1)
        gather.peer(0)
        gather.own(2)
        gather.peer(1)
        each_array(1, lambda i, which: lend(i, which).start())
        gather.own(3)
        gather.peer(2)
        gather.peer(3)
        each(0, tiles, find)
        stack(0)
        gather.natives(0)
        stack(1)
        gather.ready(0)
        weave(score(0, 0))
        weave(score(0, 1), weigh(0, 0))
        gather.natives(1)
        weave(value_part(0, 0), weigh(0, 1))
        weave(value_part(0, 1))
        reduce.first(0)
        gather.ready(1)
        weave(score(1, 0))
        gather.natives(2)
        weave(score(1, 1), weigh(1, 0))
        weave(value_part(1, 0), weigh(1, 1))
        reduce.third(0)
        weave(value_part(1, 1))
        reduce.first(1)
        gather.natives(3)
        gather.ready(2)
        weave(key_part(0, 0))
        reduce.third(1)
        weave(key_part(0, 1))
        reduce.first(2)
        for t in range(NC):
            turn(0, t)
        finish_query(0)
        gather.ready(3)
        weave(key_part(1, 0, True))
        reduce.third(2)
        weave(key_part(1, 1, True))
        reduce.first(3)
        weave(query_part(1, 0), query_part(1, 1))
        for t in range(NC):
            turn(1, t)
        reduce.third(3)
        finish_query(1)
    else:
        each(0, tiles, find)
        for i in range(MINE):
            each_array(i, lambda i, which: lend(i, which).start())
            for q in (i, MINE + i):
                gather.own(q)
                gather.peer(q)
                gather.natives(q)
                gather.ready(q)
            stack(i)
            for t in range(NC):
                weave(score(i, t))
                weave(weigh(i, t))
                weave(value_part(i, t))
            reduce.first(i)
            for t in range(NC):
                weave(key_part(i, t))
                turn(i, t)
            finish_query(i)
            reduce.first(MINE + i)
            for r in (i, MINE + i):
                reduce.third(r)
    for r in range(STAGES):
        reduce.second(r)
    for r in range(STAGES):
        reduce.fourth(r)
    for i in range(MINE):
        keep_dq(i).wait()
        give_dq(i).wait_send()
        take_dq(i).wait_recv()
        each_array(i, lambda i, which: lend(i, which).wait_send())
    for r in range(STAGES):
        gather.drain(r)
        reduce.drain(r)


def finish_kernel(a_ref, b_ref, c_ref, x_ref, y_ref, z_ref):
    x_ref[...] = a_ref[...]
    y_ref[...] = b_ref[...]
    z_ref[...] = c_ref[...]


def per_device(tiles, queries, keys, values, outputs, out_grad, ancestors):
    depth = ancestors.shape[1]
    pairs = (depth + 1) // 2
    slots = 1 + 2 * pairs
    nz = tiles // (NY * NC)
    wide = pairs <= UNROLL
    vmem = pl.BlockSpec(memory_space=pltpu.VMEM)
    smem = pl.BlockSpec(memory_space=pltpu.SMEM)
    hbm = pl.BlockSpec(memory_space=pl.ANY)
    f32, bf16 = jnp.float32, jnp.bfloat16
    dma = pltpu.SemaphoreType.DMA
    shapes = (
        jax.ShapeDtypeStruct(queries.shape, bf16),
        jax.ShapeDtypeStruct(keys.shape, bf16),
        jax.ShapeDtypeStruct(values.shape, bf16),
    )
    results = pl.pallas_call(
        functools.partial(backward_kernel, tiles, pairs, wide),
        out_shape=shapes,
        in_specs=[smem] + [vmem] * 2 + [hbm] * 3,
        out_specs=(hbm, vmem, vmem),
        scratch_shapes=[
            pltpu.SMEM((NC, tiles), jnp.int32),
            pltpu.VMEM((NC, MINE, TILE, ROWS), bf16),
            pltpu.VMEM((NC, MINE, TILE, ROWS), bf16),
            pltpu.VMEM((NC, MINE, TILE, ROWS), bf16),
            dma((MINE, 3)), dma((MINE, 3)), dma((MINE, 3)), dma((MINE,)), dma((MINE,)), dma((MINE,)),
            pltpu.VMEM((NC, MINE, ROWS, HD), bf16),
            pltpu.VMEM((NC, MINE, ROWS, HD), bf16),
            pltpu.VMEM((NC, MINE, 1, ROWS), f32),
            pltpu.VMEM((NC * MINE if wide else NC, slots, TILE, ROWS), f32),
            pltpu.VMEM((NC, slots if wide else 1, TILE, ROWS), bf16),
            pltpu.VMEM((NC, 8, ROWS), f32),
            pltpu.VMEM((NC, 8, ROWS), f32),
            pltpu.VMEM((NC * MINE, 1, ROWS), f32),
            pltpu.VMEM((NC, HD, ROWS), f32),
            pltpu.VMEM((STAGES, NC, slots, TILE, HD), f32),
        ]
        + [pltpu.VMEM((tiles, TILE, HD), bf16)] * STAGES
        + Gather.sems(nz)
        + Reduce.scratch(nz),
        compiler_params=pltpu.CompilerParams(
            collective_id=0, has_side_effects=True, vmem_limit_bytes=62 << 20),
    )(ancestors, keys, values, queries, out_grad, outputs)
    steps = 4

    def columns(shape):
        return pl.BlockSpec((shape.shape[0], shape.shape[1] // steps), lambda i: (0, i))

    specs = tuple(columns(shape) for shape in shapes)
    return pl.pallas_call(
        finish_kernel, out_shape=shapes, grid=(steps,), in_specs=list(specs), out_specs=specs,
    )(*results)


def solution(mesh):
    rows = P(("parts", "tok"), None)
    return jax.shard_map(
        functools.partial(per_device, mesh.shape["tok"]),
        mesh=mesh,
        in_specs=(rows,) * 5 + (P("parts", None),),
        out_specs=(rows,) * 3,
        check_vma=False,
    )
```

```python
import functools
import math

import jax
import jax.numpy as jnp
from jax import lax
from jax.experimental import pallas as pl
from jax.experimental.pallas import tpu as pltpu
from jax.sharding import PartitionSpec as P

QH = 32
KVH = 4
HD = 128
TILE = 128
GROUP = QH // KVH
ROWS = GROUP * TILE
SCALE = HD ** -0.5
EXP_SCALE = SCALE * math.log2(math.e)
LOOP = lax.fori_loop
NY = 2
NC = 2
MINE = KVH // NC
STAGES = 2 * MINE
UNROLL = 6


class Place:
    def __init__(self, tiles):
        self.nz = tiles // (NY * NC)
        tok = lax.axis_index("tok")
        self.z = tok // (NY * NC)
        self.y = lax.rem(tok // NC, NY)
        self.c = lax.rem(tok, NC)
        self.below_top = self.z + 1 < self.nz
        self.next_to_top = self.z + 2 == self.nz
        self.crossing = jnp.where(self.below_top, self.z, self.z - 1)

    def tile(self, z, y, c):
        return (z * NY + y) * NC + c

    def chip(self, z, y):
        return pl.ds((z * NY + y) * NC, NC)

    def at(self, z, y, c):
        z = jnp.clip(z, 0, self.nz - 1)
        return {"tok": self.tile(z, y, c)}

    def greet_all(self):
        barrier = pltpu.get_barrier_semaphore()

        def greet(z, y, c):
            pl.semaphore_signal(barrier, 1, device_id=self.at(z, y, c))

        for c in range(NC):
            greet(self.z, 1 - self.y, c)
            for d in range(1, self.nz):
                greet(lax.rem(self.z + d, self.nz), self.y, c)
        greet(self.z, self.y, 1 - self.c)

    def meet(self):
        pl.semaphore_wait(pltpu.get_barrier_semaphore(), NC * self.nz + 1)


def each(start, stop, body):
    def step(i, carry):
        body(i)
        return carry

    LOOP(start, stop, step, 0)


class Gather:
    def __init__(self, place, own, buf, sems):
        self.p, self.own_refs, self.buf = place, own, buf
        self.os, self.rs, self.us, self.ur, self.ys, self.yr = sems

    @staticmethod
    def sems(nz):
        dma = pltpu.SemaphoreType.DMA
        return [
            dma((STAGES, NC, nz + 1)), dma((STAGES, NC, nz + 1)), dma((STAGES,)), dma((STAGES,)),
            dma((STAGES, nz)), dma((STAGES, nz)),
        ]

    def small(self, q, lane, route):
        p = self.p
        kind, i = q // MINE, q % MINE
        columns = pl.ds(pl.multiple_of((lane * MINE + i) * HD, HD), HD)
        target = p.at(p.z + route, p.y, lane) if route < p.nz else p.at(p.z, 1 - p.y, lane)
        return pltpu.make_async_remote_copy(
            self.own_refs[kind].at[:, columns], self.buf[q].at[p.tile(p.z, p.y, p.c)],
            self.os.at[q, lane, route], self.rs.at[q, p.c, route], device_id=target)

    def got_small(self, q, z, y, c, route):
        p = self.p
        block = self.buf[q].at[p.tile(z, y, c)]
        pltpu.make_async_remote_copy(
            block, block, self.us.at[q], self.rs.at[q, c, route], device_id=p.at(p.z, p.y, 1 - p.c)).wait_recv()

    def up_other(self, q, z):
        p = self.p
        block = self.buf[q].at[p.chip(z, 1 - p.y)]
        return pltpu.make_async_remote_copy(
            block, block, self.us.at[q], self.ur.at[q], device_id=p.at(z + 1, p.y, p.c))

    def across(self, q, z, y):
        p = self.p
        block = self.buf[q].at[p.chip(z, y)]
        return pltpu.make_async_remote_copy(
            block, block, self.ys.at[q, z], self.yr.at[q, z], device_id=p.at(p.z, 1 - p.y, p.c))

    def routes(self, q, act):
        p = self.p
        for lane in range(NC):
            pl.when((p.y == 0) | p.next_to_top)(lambda lane=lane: act(self.small(q, lane, p.nz)))
            pl.when(p.c != lane)(lambda lane=lane: act(self.small(q, lane, 0)))
        for d in range(p.nz - 1, 0, -1):
            for lane in range(NC):
                pl.when(p.z + d < p.nz)(lambda lane=lane, d=d: act(self.small(q, lane, d)))

    def own(self, q):
        self.routes(q, lambda copy: copy.start())

    def peer(self, q):
        p = self.p

        @pl.when((p.y == 1) | p.next_to_top)
        def _():
            for c in range(NC):
                self.got_small(q, p.z, 1 - p.y, c, p.nz)

        pl.when(p.next_to_top)(lambda: self.up_other(q, p.z).start())

    def natives(self, q):
        p = self.p

        def step(z):
            for c in range(NC):
                self.got_small(q, z, p.y, c, p.z - z)
            self.across(q, z, p.y).start()

        each(0, p.crossing, step)

    def ready(self, q):
        p = self.p
        self.got_small(q, p.z, p.y, 1 - p.c, 0)

        @pl.when(jnp.logical_not(p.below_top))
        def _():
            for c in range(NC):
                self.got_small(q, p.z - 1, p.y, c, 1)
            self.up_other(q, p.z - 1).wait_recv()

        each(0, p.crossing, lambda z: self.across(q, z, 1 - p.y).wait_recv())

    def drain(self, q):
        p = self.p
        self.routes(q, lambda copy: copy.wait_send())
        pl.when(p.next_to_top)(lambda: self.up_other(q, p.z).wait_send())
        each(0, p.crossing, lambda z: self.across(q, z, p.y).wait_send())


class Reduce:
    def __init__(self, place, part, slot_of, out, scratch):
        self.p, self.part, self.slot_of, self.out = place, part, slot_of, out
        (self.kept, self.total, self.for_y, self.from_y, self.for_z, self.from_z, self.for_other,
         self.from_other, self.ys, self.yr, self.zs, self.zr, self.us, self.ur, self.cs, self.cr) = scratch

    @staticmethod
    def scratch(nz):
        dma = pltpu.SemaphoreType.DMA
        block = (NC, TILE, HD)
        f32, bf16 = jnp.float32, jnp.bfloat16
        return [
            pltpu.VMEM((STAGES,) + block, f32),
            pltpu.VMEM((STAGES,) + block, bf16),
            pltpu.VMEM((STAGES, nz) + block, bf16),
            pltpu.VMEM((STAGES, nz) + block, bf16),
            pltpu.VMEM((STAGES, nz) + block, bf16),
            pltpu.VMEM((STAGES, nz) + block, bf16),
            pltpu.VMEM((STAGES,) + block, bf16),
            pltpu.VMEM((STAGES,) + block, bf16),
        ] + [dma((STAGES, nz))] * 4 + [dma((STAGES,))] * 4

    def to_y(self, r, z):
        p = self.p
        return pltpu.make_async_remote_copy(
            self.for_y.at[r, z], self.from_y.at[r, z], self.ys.at[r, z], self.yr.at[r, z],
            device_id=p.at(p.z, 1 - p.y, p.c))

    def down(self, r, z):
        p = self.p
        return pltpu.make_async_remote_copy(
            self.for_z.at[r, z], self.from_z.at[r, p.z], self.zs.at[r, z], self.zr.at[r, p.z],
            device_id=p.at(z, p.y, p.c))

    def came_down(self, r, z):
        p = self.p
        pltpu.make_async_remote_copy(
            self.for_z.at[r, z], self.from_z.at[r, z], self.zs.at[r, z], self.zr.at[r, z],
            device_id=p.at(z, p.y, p.c)).wait_recv()

    def down_other(self, r):
        p = self.p
        return pltpu.make_async_remote_copy(
            self.for_other.at[r], self.from_other.at[r], self.us.at[r], self.ur.at[r],
            device_id=p.at(p.z - 1, p.y, p.c))

    def hand_over(self, r):
        p = self.p
        block = self.total.at[r, 1 - p.c]
        columns = pl.ds(pl.multiple_of((p.c * MINE + r % MINE) * HD, HD), HD)
        return pltpu.make_async_remote_copy(
            block, self.out[r // MINE].at[:, columns], self.cs.at[r], self.cr.at[r],
            device_id=p.at(p.z, p.y, 1 - p.c))

    def handed(self, r):
        p = self.p
        block = self.total.at[r, p.c]
        columns = pl.ds(pl.multiple_of(((1 - p.c) * MINE + r % MINE) * HD, HD), HD)
        return pltpu.make_async_remote_copy(
            block, self.out[r // MINE].at[:, columns], self.cs.at[r], self.cr.at[r],
            device_id=p.at(p.z, p.y, 1 - p.c))

    def block(self, r, z, y, c):
        tile = self.p.tile(z, y, c)
        return self.part[r, 0, self.slot_of[0, tile]] + self.part[r, 1, self.slot_of[1, tile]]

    def first(self, r):
        p = self.p

        def cross(z):
            for c in range(NC):
                self.for_y[r, z, c] = self.block(r, z, 1 - p.y, c).astype(jnp.bfloat16)
            self.to_y(r, z).start()

        each(0, p.crossing, cross)
        pl.when((p.y == 1) & jnp.logical_not(p.next_to_top))(lambda: cross(p.z))

        @pl.when(jnp.logical_not(p.below_top))
        def _():
            for c in range(NC):
                self.for_other[r, c] = self.block(r, p.z - 1, 1 - p.y, c).astype(jnp.bfloat16)
            self.down_other(r).start()
            for c in range(NC):
                self.for_z[r, p.z - 1, c] = self.block(r, p.z - 1, p.y, c).astype(jnp.bfloat16)
            self.down(r, p.z - 1).start()

    def second(self, r):
        p = self.p

        @pl.when(p.next_to_top)
        def _():
            self.down_other(r).wait_recv()
            for c in range(NC):
                mine = jnp.where(p.y == 1, self.block(r, p.z, 1 - p.y, c), 0.0)
                self.for_y[r, p.z, c] = (mine + self.from_other[r, c].astype(jnp.float32)).astype(jnp.bfloat16)
            self.to_y(r, p.z).start()

    def third(self, r):
        p = self.p

        def step(z):
            self.to_y(r, z).wait_recv()
            for c in range(NC):
                total = self.block(r, z, p.y, c) + self.from_y[r, z, c].astype(jnp.float32)
                self.for_z[r, z, c] = total.astype(jnp.bfloat16)
            self.down(r, z).start()

        each(0, p.crossing, step)

    def fourth(self, r):
        p = self.p
        for c in range(NC):
            self.kept[r, c] = self.block(r, p.z, p.y, c)

        @pl.when((p.y == 0) | p.next_to_top)
        def _():
            self.to_y(r, p.z).wait_recv()
            self.kept[r] += self.from_y[r, p.z].astype(jnp.float32)

        def step(z):
            self.came_down(r, z)
            self.kept[r] += self.from_z[r, z].astype(jnp.float32)

        each(p.z + 1, p.nz, step)
        self.total[r] = self.kept[r].astype(jnp.bfloat16)
        self.hand_over(r).start()
        columns = pl.ds(pl.multiple_of((p.c * MINE + r % MINE) * HD, HD), HD)
        self.out[r // MINE][:, columns] = self.total[r, p.c]

    def drain(self, r):
        p = self.p
        self.handed(r).wait_recv()
        self.hand_over(r).wait_send()
        each(0, p.crossing, lambda z: self.to_y(r, z).wait_send())
        pl.when((p.y == 1) | p.next_to_top)(lambda: self.to_y(r, p.z).wait_send())
        each(0, p.z, lambda z: self.down(r, z).wait_send())
        pl.when(jnp.logical_not(p.below_top))(lambda: self.down_other(r).wait_send())


def dot(a, b):
    return jnp.dot(a, b, preferred_element_type=jnp.float32)


def dot_last(a, b):
    return lax.dot_general(
        a, b, (((1,), (1,)), ((), ())), preferred_element_type=jnp.float32)


def fold(x, op):
    return op(x.reshape(TILE // 8, 8, x.shape[-1]), axis=0)


HALVES = (slice(0, TILE), slice(TILE, 2 * TILE))


def backward_kernel(
    tiles, pairs, wide, anc, k_hbm, v_hbm, q_hbm, g_hbm, o_hbm, dq_hbm, dk_ref, dv_ref,
    slot_of, k_ref, v_ref, q_in, g_in, o_in, first_sem, load_sem, send_sem, recv_sem, store_sem, give_sem, take_sem,
    qs, gs, delta, scores, slopes, peak, total, inverse, dqt, part, *rest,
):
    place = Place(tiles)
    z, y, c = place.z, place.y, place.c
    depth = anc.shape[1]
    buf, rest = rest[:STAGES], rest[STAGES:]
    gather = Gather(place, (k_ref, v_ref), buf, rest[:6])
    reduce = Reduce(place, part, slot_of, (dv_ref, dk_ref), rest[6:])
    arrays = ((q_hbm, q_in), (g_hbm, g_in), (o_hbm, o_in))

    def slab(core, i):
        return pl.ds(pl.multiple_of((core * MINE + i) * ROWS, ROWS), ROWS)

    def load(i, which):
        src, dst = arrays[which]
        return pltpu.make_async_copy(src.at[:, slab(c, i)], dst.at[c, i], load_sem.at[i, which])

    def lend(i, which):
        src, dst = arrays[which]
        return pltpu.make_async_remote_copy(
            src.at[:, slab(1 - c, i)], dst.at[c, i], send_sem.at[i, which], recv_sem.at[i, which],
            device_id=place.at(z, y, 1 - c))

    def borrowed(i, which):
        src, dst = arrays[which]
        return pltpu.make_async_remote_copy(
            src.at[:, slab(c, i)], dst.at[1 - c, i], send_sem.at[i, which], recv_sem.at[i, which],
            device_id=place.at(z, y, 1 - c))

    def keep_dq(i):
        return pltpu.make_async_copy(q_in.at[c, i], dq_hbm.at[:, slab(c, i)], store_sem.at[i])

    def give_dq(i):
        return pltpu.make_async_remote_copy(
            q_in.at[1 - c, i], dq_hbm.at[:, slab(c, i)], give_sem.at[i], take_sem.at[i],
            device_id=place.at(z, y, 1 - c))

    def take_dq(i):
        return pltpu.make_async_remote_copy(
            q_in.at[1 - c, i], dq_hbm.at[:, slab(1 - c, i)], give_sem.at[i], take_sem.at[i],
            device_id=place.at(z, y, 1 - c))

    def each_array(i, act):
        for which in range(3):
            act(i, which)

    def me(t):
        return place.tile(z, y, t)

    def weave(*works):
        if wide:
            for n in range(-1, pairs):
                for work in works:
                    work(n)
        else:
            for work in works:
                work(-1)
                each(0, pairs, work)

    def listed(t, i):
        return jnp.where(i < depth, anc[me(t), jnp.minimum(i, depth - 1)], -1)

    def find(tile):
        for t in range(NC):
            slot = jnp.where(tile == me(t), 0, part.shape[2] - 1)
            for i in range(depth):
                slot = jnp.where(listed(t, i) == tile, i + 1, slot)
            slot_of[t, tile] = slot

    def stack(i):
        each_array(i, lambda i, which: load(i, which).wait())
        each_array(i, lambda i, which: borrowed(i, which).wait_recv())

        def step(h):
            rows = pl.ds(pl.multiple_of(h * TILE, TILE), TILE)
            for t in range(NC):
                q, go = q_in[t, i, :, rows], g_in[t, i, :, rows]
                qs[t, i, rows, :] = q
                gs[t, i, rows, :] = go
                product = go.astype(jnp.float32) * o_in[t, i, :, rows].astype(jnp.float32)
                delta[t, i, :, rows] = jnp.sum(product.T, axis=0, keepdims=True)

        each(0, GROUP, step)

    def place_of(i, t):
        return i * NC + t if wide else t

    def key_tile(i, t):
        return buf[i][me(t)]

    def tile_pair(q, t, n):
        return jnp.concatenate([buf[q][jnp.maximum(listed(t, 2 * n + j), 0)] for j in range(2)], axis=0)

    def score(i, t):
        b = place_of(i, t)

        def step(n):
            if isinstance(n, int) and n < 0:
                s = dot_last(key_tile(i, t), qs[t, i])
                key_pos = lax.broadcasted_iota(jnp.int32, s.shape, 0)
                query_pos = lax.broadcasted_iota(jnp.int32, s.shape, 1) & (TILE - 1)
                s = jnp.where(key_pos <= query_pos, s, -1e30)
                scores[b, 0] = s
                peak[t] = fold(s, jnp.max)
                return
            s = dot_last(tile_pair(i, t, n), qs[t, i])
            for j, half in enumerate(HALVES):
                scores[b, 1 + 2 * n + j] = s[half]
                bias = jnp.where(listed(t, 2 * n + j) >= 0, 0.0, -1e30)
                peak[t] = jnp.maximum(peak[t], fold(s[half], jnp.max) + bias)

        return step

    def weigh(i, t):
        b = place_of(i, t)

        def step(n):
            if isinstance(n, int) and n < 0:
                top = jnp.max(peak[t], axis=0, keepdims=True)
                inverse[b] = top
                w = jnp.exp2((scores[b, 0] - top) * EXP_SCALE)
                scores[b, 0] = w
                total[t] = fold(w, jnp.sum)
                return
            for j in range(2):
                slot = 1 + 2 * n + j
                top = inverse[b] + jnp.where(listed(t, 2 * n + j) >= 0, 0.0, 1e30)
                w = jnp.exp2((scores[b, slot] - top) * EXP_SCALE)
                scores[b, slot] = w
                total[t] += fold(w, jnp.sum)

        return step

    def value_part(i, t):
        b = place_of(i, t)

        def step(n):
            if isinstance(n, int) and n < 0:
                inverse[b] = 1.0 / jnp.sum(total[t], axis=0, keepdims=True)
                part[i, t, 0] = dot((scores[b, 0] * inverse[b]).astype(jnp.bfloat16), gs[t, i])
                return
            first = 1 + 2 * n
            p = scores[b, pl.ds(first, 2)].reshape(2 * TILE, ROWS) * inverse[b]
            dv = dot(p.astype(jnp.bfloat16), gs[t, i])
            for j, half in enumerate(HALVES):
                part[i, t, first + j] = dv[half]

        return step

    def key_part(i, t, later=False):
        b = place_of(i, t)
        q = MINE + i

        def step(n):
            if isinstance(n, int) and n < 0:
                slope = dot_last(buf[q][me(t)], gs[t, i]) - delta[t, i]
                ds = (scores[b, 0] * inverse[b] * slope).astype(jnp.bfloat16)
                part[q, t, 0] = dot(ds, qs[t, i]) * SCALE
                if later:
                    slopes[b, 0] = ds
                else:
                    dqt[t] = dot(key_tile(i, t).T, ds)
                return
            first = 1 + 2 * n
            slope = dot_last(tile_pair(q, t, n), gs[t, i]) - delta[t, i]
            p = scores[b, pl.ds(first, 2)].reshape(2 * TILE, ROWS) * inverse[b]
            ds = (p * slope).astype(jnp.bfloat16)
            dk = dot(ds, qs[t, i]) * SCALE
            for j, half in enumerate(HALVES):
                part[q, t, first + j] = dk[half]
                if later:
                    slopes[b, first + j] = ds[half]
            if not later:
                dqt[t] += dot(tile_pair(i, t, n).T, ds)

        return step

    def query_part(i, t):
        b = place_of(i, t)

        def step(n):
            if isinstance(n, int) and n < 0:
                dqt[t] = dot(key_tile(i, t).T, slopes[b, 0])
                return
            ds = slopes[b, pl.ds(1 + 2 * n, 2)].reshape(2 * TILE, ROWS)
            dqt[t] += dot(tile_pair(i, t, n).T, ds)

        return step

    def turn(i, t):
        for h in range(GROUP):
            rows = slice(h * TILE, (h + 1) * TILE)
            q_in[t, i, :, rows] = (dqt[t, :, rows].T * SCALE).astype(jnp.bfloat16)

    first_loads = (
        pltpu.make_async_copy(k_hbm, k_ref, first_sem.at[0]), pltpu.make_async_copy(v_hbm, v_ref, first_sem.at[1]),
    )
    for copy in first_loads:
        copy.start()
    place.greet_all()
    each_array(0, lambda i, which: load(i, which).start())
    each_array(1, lambda i, which: load(i, which).start())
    for r in range(STAGES):
        for t in range(NC):
            part[r, t, part.shape[2] - 1] = jnp.zeros((TILE, HD), jnp.float32)
    for copy in first_loads:
        copy.wait()
    for i in range(MINE):
        columns = pl.ds(pl.multiple_of((c * MINE + i) * HD, HD), HD)
        buf[i][me(c)] = k_ref[:, columns]
        buf[MINE + i][me(c)] = v_ref[:, columns]
    place.meet()

    def finish_query(i):
        keep_dq(i).start()
        give_dq(i).start()

    if wide:
        gather.own(0)
        each_array(0, lambda i, which: lend(i, which).start())
        gather.own(1)
        gather.peer(0)
        gather.own(2)
        gather.peer(1)
        each_array(1, lambda i, which: lend(i, which).start())
        gather.own(3)
        gather.peer(2)
        gather.peer(3)
        each(0, tiles, find)
        stack(0)
        gather.natives(0)
        gather.ready(0)
        weave(score(0, 0))
        weave(score(0, 1), weigh(0, 0))
        gather.natives(1)
        weave(value_part(0, 0), weigh(0, 1))
        weave(value_part(0, 1))
        reduce.first(0)
        stack(1)
        gather.ready(1)
        weave(score(1, 0))
        gather.natives(2)
        weave(score(1, 1), weigh(1, 0))
        weave(value_part(1, 0), weigh(1, 1))
        reduce.third(0)
        weave(value_part(1, 1))
        reduce.first(1)
        gather.natives(3)
        gather.ready(2)
        weave(key_part(0, 0, True))
        reduce.third(1)
        weave(key_part(0, 1, True))
        reduce.first(2)
        reduce.second(0)
        gather.ready(3)
        weave(key_part(1, 0, True))
        reduce.third(2)
        weave(key_part(1, 1, True))
        reduce.first(3)
        reduce.second(1)
        reduce.second(2)
        weave(query_part(0, 0), query_part(0, 1))
        for t in range(NC):
            turn(0, t)
        finish_query(0)
        reduce.third(3)
        reduce.second(3)
        weave(query_part(1, 0), query_part(1, 1))
        for t in range(NC):
            turn(1, t)
        finish_query(1)
    else:
        each(0, tiles, find)
        for i in range(MINE):
            each_array(i, lambda i, which: lend(i, which).start())
            for q in (i, MINE + i):
                gather.own(q)
                gather.peer(q)
                gather.natives(q)
                gather.ready(q)
            stack(i)
            for t in range(NC):
                weave(score(i, t))
                weave(weigh(i, t))
                weave(value_part(i, t))
            reduce.first(i)
            for t in range(NC):
                weave(key_part(i, t))
                turn(i, t)
            finish_query(i)
            reduce.first(MINE + i)
            for r in (i, MINE + i):
                reduce.third(r)
                reduce.second(r)
    for r in range(STAGES):
        reduce.fourth(r)
    for i in range(MINE):
        keep_dq(i).wait()
        give_dq(i).wait_send()
        take_dq(i).wait_recv()
        each_array(i, lambda i, which: lend(i, which).wait_send())
    for r in range(STAGES):
        gather.drain(r)
        reduce.drain(r)


def finish_kernel(steps, *refs):
    given, results, held, sems = refs[:3], refs[3:6], refs[6:9], refs[9]

    def copies(i, n):
        height = given[i].shape[0] // steps
        rows = pl.ds(n * height, height)
        return (
            pltpu.make_async_copy(given[i].at[rows], held[i].at[rows], sems.at[0, i, n]),
            pltpu.make_async_copy(held[i].at[rows], results[i].at[rows], sems.at[1, i, n]),
        )

    every = [copies(i, n) for n in range(steps) for i in range(3)]
    for into, _ in every:
        into.start()
    for into, out in every:
        into.wait()
        out.start()
    for _, out in every:
        out.wait()


def per_device(tiles, queries, keys, values, outputs, out_grad, ancestors):
    depth = ancestors.shape[1]
    pairs = (depth + 1) // 2
    slots = 1 + 2 * pairs
    nz = tiles // (NY * NC)
    wide = pairs <= UNROLL
    vmem = pl.BlockSpec(memory_space=pltpu.VMEM)
    smem = pl.BlockSpec(memory_space=pltpu.SMEM)
    hbm = pl.BlockSpec(memory_space=pl.ANY)
    f32, bf16 = jnp.float32, jnp.bfloat16
    dma = pltpu.SemaphoreType.DMA
    shapes = (
        jax.ShapeDtypeStruct(queries.shape, bf16),
        jax.ShapeDtypeStruct(keys.shape, bf16),
        jax.ShapeDtypeStruct(values.shape, bf16),
    )
    results = pl.pallas_call(
        functools.partial(backward_kernel, tiles, pairs, wide),
        out_shape=shapes,
        in_specs=[smem] + [hbm] * 5,
        out_specs=(hbm, vmem, vmem),
        scratch_shapes=[
            pltpu.SMEM((NC, tiles), jnp.int32),
            pltpu.VMEM(keys.shape, bf16),
            pltpu.VMEM(values.shape, bf16),
            pltpu.VMEM((NC, MINE, TILE, ROWS), bf16),
            pltpu.VMEM((NC, MINE, TILE, ROWS), bf16),
            pltpu.VMEM((NC, MINE, TILE, ROWS), bf16),
            dma((2,)), dma((MINE, 3)), dma((MINE, 3)), dma((MINE, 3)), dma((MINE,)), dma((MINE,)), dma((MINE,)),
            pltpu.VMEM((NC, MINE, ROWS, HD), bf16),
            pltpu.VMEM((NC, MINE, ROWS, HD), bf16),
            pltpu.VMEM((NC, MINE, 1, ROWS), f32),
            pltpu.VMEM((NC * MINE if wide else NC, slots, TILE, ROWS), f32),
            pltpu.VMEM((NC * MINE if wide else 1, slots if wide else 1, TILE, ROWS), bf16),
            pltpu.VMEM((NC, 8, ROWS), f32),
            pltpu.VMEM((NC, 8, ROWS), f32),
            pltpu.VMEM((NC * MINE, 1, ROWS), f32),
            pltpu.VMEM((NC, HD, ROWS), f32),
            pltpu.VMEM((STAGES, NC, slots + 1, TILE, HD), f32),
        ]
        + [pltpu.VMEM((tiles, TILE, HD), bf16)] * STAGES
        + Gather.sems(nz)
        + Reduce.scratch(nz),
        compiler_params=pltpu.CompilerParams(
            collective_id=0, has_side_effects=True, vmem_limit_bytes=62 << 20),
    )(ancestors, keys, values, queries, out_grad, outputs)
    steps = 4
    return pl.pallas_call(
        functools.partial(finish_kernel, steps), out_shape=shapes, in_specs=[hbm] * 3, out_specs=(hbm,) * 3,
        scratch_shapes=[pltpu.VMEM(shape.shape, bf16) for shape in shapes] + [dma((2, 3, steps))],
    )(*results)


def solution(mesh):
    rows = P(("parts", "tok"), None)
    return jax.shard_map(
        functools.partial(per_device, mesh.shape["tok"]),
        mesh=mesh,
        in_specs=(rows,) * 5 + (P("parts", None),),
        out_specs=(rows,) * 3,
        check_vma=False,
    )
```
